128 devices in a mesh: tm: 8 (over x, core), space: 16 (over z, y).
Axes of the slice: x: 4, y: 4, z: 4, core: 2. Of those that a mesh axis runs over, the one named last changes fastest.
Arguments:
- field: float32 [4096, 128, 256], P('tm', 'space'), may hold values from -6 to 6
- mask: int32 [4096, 128, 256], P('tm', 'space'), may hold values 0 or 1
- noise: float32 [128, 256], P('space'), may hold values from 0.1 to 1
- lat_factor: float32 [128, 128], replicated, may hold values from -1 to 2.5, as said below
- lon_factor: float32 [256, 256], replicated, may hold values from -1 to 2.5, as said below
- time_tiles: float32 [5, 128, 128], replicated, may hold values from -1 to 2.5, as said below
- amplitude: float32 [32], replicated, may hold values from 0.5 to 2
- depth: int32 [32], replicated, may hold values from 0 to 4
Outputs:
- product: float32 [4096, 128, 256], P('tm', 'space')
The draws below stay inside these ranges and needn't reach their ends.
Inputs may be any that keep to these rules, and one draw needn't show every extreme that they name: `lat_factor`: symmetric. `lon_factor`: symmetric. time_tiles[0] is symmetric.
All inputs are finite; a program needn't handle non-finite values. No bound on the sum of `mask` on one device may be relied on, other than what follows from the above.
Results may differ from the reference program's by a relative error of at most 0.0001.
Values sent between devices are 32-bit elements; how exact they have to be, the bound alone decides.
A program may use at most 192 MiB of HBM per device.

```python
import math
import jax
import jax.numpy as jnp
from jax import lax

LAT = 128
LON = 256
HB = 128
NBLK = 32
HOURS = 4096


def symmetric_factor(key, order):
    noise_part = jax.random.normal(key, (order, order), jnp.float32) / jnp.sqrt(order * 1.0)
    result = jnp.eye(order, dtype=jnp.float32) + 0.3 * (noise_part + noise_part.T)
    return jnp.clip(result, -1.0, 2.5)


def draw_lat_factor(key, part):
    return symmetric_factor(jax.random.fold_in(key, 11), LAT)


def draw_lon_factor(key, part):
    return symmetric_factor(jax.random.fold_in(key, 13), LON)


def draw_time_tiles(key, part):
    diagonal_tile = symmetric_factor(jax.random.fold_in(key, 21), HB)
    others = 0.5 * jax.random.normal(jax.random.fold_in(key, 22), (4, HB, HB), jnp.float32) / jnp.sqrt(HB * 1.0)
    others = jnp.clip(others, -1.0, 2.5)
    return jnp.concatenate([diagonal_tile[None], others], axis=0)


def with_ends(entries, key, least, top_value):
    longest = entries.shape.index(max(entries.shape))
    spots = []
    for shift in (0, 1):
        where = [jax.random.randint(jax.random.fold_in(key, axis), (), 0, length) for axis, length in enumerate(entries.shape)]
        where[longest] = (where[longest] + shift) % entries.shape[longest]
        spots.append(tuple(where))
    return entries.at[spots[0]].set(least).at[spots[1]].set(top_value)


def shard_levels(own_key, dims, shards, least, top_value):
    factor_of, own = 1.0, jax.random.fold_in(own_key, 6)
    for position, blocks in shards:
        steps = jnp.exp(jax.random.uniform(jax.random.fold_in(own, position), (blocks,), jnp.float32, least / len(shards), top_value / len(shards)))
        factor_of = factor_of * jnp.repeat(steps, dims[position] // blocks).reshape([-1 if axis == position else 1 for axis in range(len(dims))])
    return factor_of


def gaussian(stream_key, shape, deviation, bound, pieces=(), kind=jnp.bfloat16):
    drawn = jax.random.normal(stream_key, shape, jnp.float32) * deviation
    if len(pieces) > 0:
        drawn = shard_levels(stream_key, shape, pieces, -0.22, 0.18) * drawn
    return jnp.clip(drawn, min=-bound, max=bound).astype(kind)


def setup_inputs(seed: int = 0) -> dict:
    arg_keys = jax.random.split(jax.random.key(seed), 9)
    field = gaussian(arg_keys[0], (HOURS, LAT, LON), 1.0, 6.0, ((0, 8), (1, 16)), jnp.float32)
    mask = with_ends((jax.random.randint(arg_keys[1], (HOURS, LAT, LON), 0, 4) < 3).astype(jnp.int32), jax.random.fold_in(arg_keys[1], 1), 0, 1)
    noise = jnp.clip(jnp.exp(math.log(1.0) - 2.3025851 * jax.random.uniform(arg_keys[2], (LAT, LON), jnp.float32) ** shard_levels(arg_keys[2], (LAT, LON), ((0, 16),), -0.2, 0.2)), 0.1, 1.0)
    lat_factor = draw_lat_factor(jax.random.fold_in(arg_keys[8], 71), 0)
    lon_factor = draw_lon_factor(jax.random.fold_in(arg_keys[8], 71), 0)
    time_tiles = draw_time_tiles(jax.random.fold_in(arg_keys[8], 71), 0)
    amplitude = jnp.clip(jnp.exp(jax.random.uniform(arg_keys[6], (NBLK,), jnp.float32, math.log(0.5), math.log(2.0))), 0.5, 2.0)
    depth = with_ends(jax.random.randint(arg_keys[7], (NBLK,), 0, 5), jax.random.fold_in(arg_keys[7], 1), 0, 4).astype(jnp.int32)
    return {"field": field, "mask": mask, "noise": noise, "lat_factor": lat_factor, "lon_factor": lon_factor, "time_tiles": time_tiles, "amplitude": amplitude, "depth": depth}


def band(padded, depth_pad, first_block, block_count, time_tiles):
    highest = lax.Precision.HIGHEST
    result = jnp.einsum("ij,bjs->bis", time_tiles[0], padded[4:4 + block_count], precision=highest)
    for offset in range(1, 5):
        depth_here = lax.dynamic_slice_in_dim(depth_pad, first_block + 4, block_count)
        depth_before = lax.dynamic_slice_in_dim(depth_pad, first_block + 4 - offset, block_count)
        weight_above = (depth_here >= offset).astype(jnp.float32)
        weight_below = (depth_before >= offset).astype(jnp.float32)
        above_term = jnp.einsum("ij,bjs->bis", time_tiles[offset], padded[4 + offset:4 + offset + block_count], precision=highest)
        below_term = jnp.einsum("ji,bjs->bis", time_tiles[offset], padded[4 - offset:4 - offset + block_count], precision=highest)
        result = result + weight_above[:, None, None] * above_term + weight_below[:, None, None] * below_term
    return result


def reference(field, mask, noise, lat_factor, lon_factor, time_tiles, amplitude, depth):
    highest = lax.Precision.HIGHEST
    masked = mask.astype(jnp.float32) * field
    rows_done = jnp.einsum("him,lm->hil", masked, lon_factor, precision=highest)
    columns = jnp.einsum("ij,hjl->hil", lat_factor, rows_done, precision=highest)
    blocks = HOURS // HB
    scaled = columns.reshape(blocks, HB, LAT * LON) * amplitude[:, None, None]
    padded = jnp.pad(scaled, ((4, 4), (0, 0), (0, 0)))
    depth_pad = jnp.pad(depth, 4)
    banded = band(padded, depth_pad, 0, blocks, time_tiles) * amplitude[:, None, None]
    banded = banded.reshape(HOURS, LAT, LON)
    return mask.astype(jnp.float32) * banded + noise[None] * field
```

```python
import functools

import jax
import jax.numpy as jnp
from jax import lax
from jax.experimental import pallas as pl
from jax.experimental.pallas import tpu as pltpu
from jax.sharding import PartitionSpec as P

MESH = pl.DeviceIdType.MESH
F32 = jnp.float32
BF16 = jnp.bfloat16
C = 8
HB = 128
OFFSETS = [(dy, dz) for dz in range(4) for dy in range(4) if (dy, dz) != (0, 0)]


def split(x):
    hi = x.astype(BF16)
    return hi, (x - hi.astype(F32)).astype(BF16)


def dot(a, b):
    return jnp.dot(a, b, preferred_element_type=F32)


def kernel(
    field, mask, noise, lat, lon, tiles, amp, depth, out,
    fbuf, mbuf, a_buf, r_buf, z_buf, y_buf, halo, acc, weights, stage, lon2, lat2,
    field_sem, mask_sem, fwd_send, fwd_recv, back_send, back_recv, halo_send, halo_recv, out_sem,
):
    t = lax.axis_index("tm")
    s = lax.axis_index("space")
    sz, sy = s // 4, s % 4
    peers = [
        lax.rem(sz + dz, 4) * 4 + lax.rem(sy + dy, 4) for dy, dz in OFFSETS
    ]
    right, left = lax.rem(t + 1, 8), lax.rem(t + 7, 8)
    rows = fbuf.shape[1]
    chunk = rows // C
    piece = chunk // 16

    def load(c):
        part = pl.ds(c * chunk, chunk)
        return [
            pltpu.make_async_copy(
                source.at[part, pl.ds(half * 128, 128)], target.at[half, part], sem.at[half, c]
            )
            for source, target, sem in ((field, fbuf, field_sem), (mask, mbuf, mask_sem))
            for half in range(2)
        ]

    for c in range(C):
        for copy in load(c):
            copy.start()

    barrier = pltpu.get_barrier_semaphore()
    for peer in peers:
        pl.semaphore_signal(barrier, inc=1, device_id=(t, peer), device_id_type=MESH)
    for side in (left, right):
        pl.semaphore_signal(barrier, inc=1, device_id=(side, s), device_id_type=MESH)

    hi, lo = split(lon[...])
    lon2[0] = hi
    lon2[1] = lo
    hi, lo = split(lat[...])
    lat2[:, 0:128] = hi
    lat2[:, 128:256] = lo
    pl.semaphore_wait(barrier, len(peers) + 2)

    @pl.loop(0, C)
    def _(c):
        for copy in load(c):
            copy.wait()
        part = pl.ds(pl.multiple_of(c * chunk, chunk), chunk)
        x = jnp.concatenate(
            [mbuf[half, part, :].astype(F32) * fbuf[half, part, :] for half in range(2)], axis=1
        )
        hi, lo = split(x)
        x = dot(hi, lon2[0]) + dot(hi, lon2[1]) + dot(lo, lon2[0])
        for half in range(2):
            a_buf[c, :, half] = x[:, half * 128 : half * 128 + 128].reshape(16, piece, 128)
        for peer in peers:
            pltpu.make_async_remote_copy(
                a_buf.at[c, peer],
                r_buf.at[c, s],
                fwd_send.at[c],
                fwd_recv.at[c],
                device_id=(t, peer),
                device_id_type=MESH,
            ).start()
        pltpu.make_async_copy(a_buf.at[c, s], r_buf.at[c, s], fwd_recv.at[c]).start()

    for side in range(3):
        for j in range(4):
            for i in range(4):
                shift = j - i + (0, -4, 4)[side]
                place = pl.ds(i * HB, HB)
                if abs(shift) > 4:
                    weights[side, j, place, :] = jnp.zeros((HB, 2 * HB), BF16)
                    continue
                to = t * 4 + i
                source = to + shift
                inside = (source >= 0) & (source <= 31)
                source = jnp.clip(source, 0, 31)
                low = jnp.minimum(to, source)
                keep = inside & (abs(shift) <= depth[low])
                factor = jnp.where(keep, amp[to] * amp[source], 0.0)
                tile = tiles[abs(shift)]
                if shift < 0:
                    tile = tile.T
                hi, lo = split(factor * tile)
                weights[side, j, place, 0:HB] = hi
                weights[side, j, place, HB : 2 * HB] = lo

    @pl.loop(0, C)
    def _(c):
        pltpu.make_async_copy(r_buf.at[c], r_buf.at[c], fwd_recv.at[c]).wait()
        for h in range(piece // 8):
            x = jnp.concatenate(
                [r_buf[c, :, half, pl.ds(h * 8, 8), :].reshape(128, 128) for half in range(2)], axis=1
            )
            hi, lo = split(x)
            both = jnp.concatenate([hi, hi], axis=0)
            y = dot(lat2[...], both) + dot(lat2[:, 0:128], lo)
            for half in range(2):
                part = y[:, half * 128 : half * 128 + 128]
                z_buf[c, :, half, pl.ds(h * 8, 8), :] = part.reshape(16, 8, 128)
        land = pl.ds(c * chunk + s * piece, piece)
        for peer in peers:
            pltpu.make_async_remote_copy(
                z_buf.at[c, peer],
                y_buf.at[:, land],
                back_send.at[c],
                back_recv.at[c],
                device_id=(t, peer),
                device_id_type=MESH,
            ).start()
        pltpu.make_async_copy(z_buf.at[c, s], y_buf.at[:, land], back_recv.at[c]).start()

    acc[...] = jnp.zeros_like(acc)

    def halo_copy(c, side):
        part = pl.ds(c * chunk, chunk)
        return pltpu.make_async_remote_copy(
            y_buf.at[:, part],
            halo.at[side, :, part],
            halo_send.at[side, c],
            halo_recv.at[side, c],
            device_id=((right, left)[side], s),
            device_id_type=MESH,
        )

    def arrived(c):
        part = pl.ds(c * chunk, chunk)
        pltpu.make_async_copy(y_buf.at[:, part], y_buf.at[:, part], back_recv.at[c]).wait()
        for side in range(2):
            halo_copy(c, side).start()

    def product(ref, side, j, r):
        x = jnp.concatenate(
            [ref[half, pl.ds(j * (HB * 8) + r, HB, stride=8), :] for half in range(2)], axis=1
        )
        hi, lo = split(x)
        both = jnp.concatenate([hi, hi], axis=0)
        return dot(weights[side, j], both) + dot(weights[side, j, :, 0:HB], lo)

    for j in range(4):
        arrived(2 * j)
        arrived(2 * j + 1)
        if j > 0:
            for c in (2 * j - 2, 2 * j - 1):
                for side in range(2):
                    halo_copy(c, side).wait_recv()

        @pl.loop(0, 8)
        def _(r, j=j):
            total = acc[r] + product(y_buf, 0, j, r)
            if j > 0:
                total += product(halo.at[0], 1, j - 1, r) + product(halo.at[1], 2, j - 1, r)
            acc[r] = total

    for c in (6, 7):
        for side in range(2):
            halo_copy(c, side).wait_recv()

    @pl.loop(0, 8)
    def _(r):
        total = acc[r] + product(halo.at[0], 1, 3, r) + product(halo.at[1], 2, 3, r)
        every = pl.ds(r, rows // 8, stride=8)
        row = lax.broadcasted_iota(jnp.int32, (8, 256), 0)
        noise_row = jnp.sum(jnp.where(row == r, noise[...], 0.0), axis=0, keepdims=True)
        for half in range(2):
            lanes = slice(half * 128, half * 128 + 128)
            stage[half, every, :] = (
                mbuf[half, every, :].astype(F32) * total[:, lanes]
                + noise_row[:, lanes] * fbuf[half, every, :]
            )

    def store(half):
        return pltpu.make_async_copy(
            stage.at[half], out.at[:, pl.ds(half * 128, 128)], out_sem.at[half]
        )

    for half in range(2):
        store(half).start()

    @pl.loop(0, C)
    def _(c):
        sent = a_buf.at[c, pl.ds(0, 15)]
        pltpu.make_async_copy(sent, sent, fwd_send.at[c]).wait()
        pltpu.make_async_copy(sent, sent, back_send.at[c]).wait()
        for side in range(2):
            halo_copy(c, side).wait_send()

    for half in range(2):
        store(half).wait()


def per_device(field, mask, noise, lat_factor, lon_factor, time_tiles, amplitude, depth):
    hours, lats, lons = field.shape
    rows = hours * lats
    piece = rows // C // 16
    anywhere = pl.BlockSpec(memory_space=pl.ANY)
    vmem = pl.BlockSpec(memory_space=pltpu.VMEM)
    smem = pl.BlockSpec(memory_space=pltpu.SMEM)
    dma = pltpu.SemaphoreType.DMA
    result = pl.pallas_call(
        kernel,
        out_shape=jax.ShapeDtypeStruct((rows, lons), F32),
        in_specs=[anywhere, anywhere, vmem, vmem, vmem, vmem, smem, smem],
        out_specs=anywhere,
        scratch_shapes=[
            pltpu.VMEM((2, rows, 128), F32),
            pltpu.VMEM((2, rows, 128), jnp.int32),
            pltpu.VMEM((C, 16, 2, piece, 128), F32),
            pltpu.VMEM((C, 16, 2, piece, 128), F32),
            pltpu.VMEM((C, 16, 2, piece, 128), F32),
            pltpu.VMEM((2, rows, 128), F32),
            pltpu.VMEM((2, 2, rows, 128), F32),
            pltpu.VMEM((lats, hours, lons), F32),
            pltpu.VMEM((3, 4, hours, 2 * HB), BF16),
            pltpu.VMEM((2, rows, 128), F32),
            pltpu.VMEM((2, lons, lons), BF16),
            pltpu.VMEM((128, 256), BF16),
            dma((2, C)), dma((2, C)), dma((C,)), dma((C,)), dma((C,)), dma((C,)),
            dma((2, C)), dma((2, C)), dma((2,)),
        ],
        compiler_params=pltpu.CompilerParams(
            collective_id=0, has_side_effects=True, vmem_limit_bytes=60 << 20
        ),
    )(
        field.reshape(rows, lons), mask.reshape(rows, lons), noise,
        lat_factor, lon_factor, time_tiles, amplitude, depth,
    )
    return result.reshape(hours, lats, lons)


def solution(mesh):
    spread = P("tm", "space", None)
    in_specs = (spread, spread, P("space", None), P(), P(), P(), P(), P())
    return jax.shard_map(
        per_device, mesh=mesh, in_specs=in_specs, out_specs=spread, check_vma=False
    )
```

```python
import jax
import jax.numpy as jnp
from jax import lax
from jax.experimental import pallas as pl
from jax.experimental.pallas import tpu as pltpu
from jax.sharding import PartitionSpec as P

MESH = pl.DeviceIdType.MESH
F32 = jnp.float32
BF16 = jnp.bfloat16
C = 4
HB = 128
OFFSETS = [(dy, dz) for dz in range(4) for dy in range(4) if (dy, dz) != (0, 0)]


def split(x):
    hi = x.astype(BF16)
    return hi, (x - hi.astype(F32)).astype(BF16)


def dot(a, b):
    return jnp.dot(a, b, preferred_element_type=F32)


def kernel(
    field, mask, noise, lat, lon, tiles, amp, depth, out,
    fbuf, mbuf, first, mixed, r_buf, z_buf, wide, y_buf, wh, wl, xh, xl, lon2, lat2,
    field_sem, mask_sem, fwd_send, fwd_recv, back_send, back_recv, halo_send, halo_recv,
):
    t = lax.axis_index("tm")
    s = lax.axis_index("space")
    sz, sy = s // 4, s % 4
    peers = [lax.rem(sz + dz, 4) * 4 + lax.rem(sy + dy, 4) for dy, dz in OFFSETS]
    right, left = lax.rem(t + 1, 8), lax.rem(t + 7, 8)
    rows = fbuf.shape[0]
    chunk = rows // C
    piece = chunk // 16

    def load(c):
        part = pl.ds(c * chunk, chunk)
        return (
            pltpu.make_async_copy(field.at[part], fbuf.at[part], field_sem.at[c]),
            pltpu.make_async_copy(mask.at[part], mbuf.at[part], mask_sem.at[c]),
        )

    for c in range(C):
        for copy in load(c):
            copy.start()

    barrier = pltpu.get_barrier_semaphore()
    for peer in peers:
        pl.semaphore_signal(barrier, inc=1, device_id=(t, peer), device_id_type=MESH)
    for side in (left, right):
        pl.semaphore_signal(barrier, inc=1, device_id=(side, s), device_id_type=MESH)

    hi, lo = split(lon[...])
    lon2[0] = hi
    lon2[1] = lo
    hi, lo = split(lat[...])
    lat2[:, 0:128] = hi
    lat2[:, 128:256] = lo

    def lon_product(c):
        for copy in load(c):
            copy.wait()
        part = pl.ds(pl.multiple_of(c * chunk, chunk), chunk)
        hi, lo = split(mbuf[part, :].astype(F32) * fbuf[part, :])
        x = dot(hi, lon2[0]) + dot(hi, lon2[1]) + dot(lo, lon2[0])
        first[part, :] = x[:, 0:128]
        wide[1, pl.ds(pl.multiple_of(rows + c * chunk, chunk), chunk), :] = x[:, 128:256]

    def send_forward(half, c):
        source = (first, mixed)[half]
        for peer in peers:
            pltpu.make_async_remote_copy(
                source.at[pl.ds((c * 16 + peer) * piece, piece)],
                r_buf.at[half, c, s],
                fwd_send.at[half, c],
                fwd_recv.at[half, c],
                device_id=(t, peer),
                device_id_type=MESH,
            ).start()
        pltpu.make_async_copy(
            source.at[pl.ds((c * 16 + s) * piece, piece)], r_buf.at[half, c, s], fwd_recv.at[half, c]
        ).start()

    def lat_product(half, c):
        got = r_buf.at[half, c]
        pltpu.make_async_copy(got, got, fwd_recv.at[half, c]).wait()
        for h in range(0, piece // 8, 2):
            x = jnp.concatenate(
                [r_buf[half, c, :, pl.ds((h + k) * 8, 8), :].reshape(128, 128) for k in range(2)], axis=1
            )
            hi, lo = split(x)
            y = dot(lat2[...], jnp.concatenate([hi, hi], axis=0)) + dot(lat2[:, 0:128], lo)
            for k in range(2):
                part = y[:, k * 128 : k * 128 + 128]
                z_buf[half, c, :, pl.ds((h + k) * 8, 8), :] = part.reshape(16, 8, 128)
        place = (c * 16 + s) * piece
        target = (wide.at[0, pl.ds(rows + place, piece)], y_buf.at[1, pl.ds(place, piece)])[half]
        for peer in peers:
            pltpu.make_async_remote_copy(
                z_buf.at[half, c, peer],
                target,
                back_send.at[half, c],
                back_recv.at[half, c],
                device_id=(t, peer),
                device_id_type=MESH,
            ).start()
        pltpu.make_async_copy(z_buf.at[half, c, s], target, back_recv.at[half, c]).start()

    def halo_copy(half, c, side):
        return pltpu.make_async_remote_copy(
            wide.at[half, pl.ds(rows + c * chunk, chunk)],
            wide.at[half, pl.ds(2 * side * rows + c * chunk, chunk)],
            halo_send.at[half, side, c],
            halo_recv.at[half, side, c],
            device_id=((right, left)[side], s),
            device_id_type=MESH,
        )

    def time_product(half):
        for c in range(C):
            for side in range(2):
                halo_copy(half, c, side).wait_recv()

        @pl.loop(0, 4)
        def _(p):
            for g in range(12):
                x = jnp.concatenate(
                    [wide[half, pl.ds(g * (HB * 8) + 2 * p + k, HB, stride=8), :] for k in range(2)], axis=1
                )
                hi, lo = split(x)
                xh[pl.ds(g * HB, HB), :] = hi
                xl[pl.ds(g * HB, HB), :] = lo
            x = dot(wh[...], xh[...]) + dot(wl[...], xh[...]) + dot(wh[...], xl[...])
            for k in range(2):
                every = pl.ds(2 * p + k, rows // 8, stride=8)
                part = x[:, k * 128 : k * 128 + 128]
                if half == 0:
                    y_buf[0, every, :] = part
                else:
                    mixed[every, :] = part

    def finish(half, c):
        part = pl.ds(pl.multiple_of(c * chunk, chunk), chunk)
        lanes = slice(half * 128, half * 128 + 128)
        tall = (chunk // 8, 8, 128)
        value = mbuf[part, lanes].astype(F32) * y_buf[half, part, :]
        value = value.reshape(tall) + noise[:, lanes][None] * fbuf[part, lanes].reshape(tall)
        out[part, lanes] = value.reshape(chunk, 128)

    lon_product(0)
    pl.semaphore_wait(barrier, len(peers) + 2)
    send_forward(0, 0)
    for side in range(2):
        halo_copy(1, 0, side).start()

    @pl.loop(1, C)
    def _(c):
        lon_product(c)
        send_forward(0, c)
        for side in range(2):
            halo_copy(1, c, side).start()

    for j in range(12):
        for i in range(4):
            shift = j - 4 - i
            place, across = pl.ds(i * HB, HB), pl.ds(j * HB, HB)
            if abs(shift) > 4:
                wh[place, across] = jnp.zeros((HB, HB), BF16)
                wl[place, across] = jnp.zeros((HB, HB), BF16)
                continue
            to = t * 4 + i
            source = to + shift
            inside = (source >= 0) & (source <= 31)
            source = jnp.clip(source, 0, 31)
            keep = inside & (abs(shift) <= depth[jnp.minimum(to, source)])
            factor = jnp.where(keep, amp[to] * amp[source], 0.0)
            tile = tiles[abs(shift)]
            if shift < 0:
                tile = tile.T
            wh[place, across], wl[place, across] = split(factor * tile)

    @pl.loop(0, C)
    def _(c):
        lat_product(0, c)

    time_product(1)

    @pl.loop(0, C)
    def _(c):
        send_forward(1, c)

    @pl.loop(0, C)
    def _(c):
        got = wide.at[0, pl.ds(rows + c * chunk, chunk)]
        pltpu.make_async_copy(got, got, back_recv.at[0, c]).wait()
        for side in range(2):
            halo_copy(0, c, side).start()

    @pl.loop(0, C)
    def _(c):
        lat_product(1, c)

    time_product(0)

    @pl.loop(0, C)
    def _(c):
        finish(0, c)

    @pl.loop(0, C)
    def _(c):
        got = y_buf.at[1, pl.ds(c * chunk, chunk)]
        pltpu.make_async_copy(got, got, back_recv.at[1, c]).wait()
        finish(1, c)

    @pl.loop(0, C)
    def _(c):
        for half in range(2):
            sent = z_buf.at[half, c, pl.ds(0, 15)]
            pltpu.make_async_copy(sent, sent, fwd_send.at[half, c]).wait()
            pltpu.make_async_copy(sent, sent, back_send.at[half, c]).wait()
            for side in range(2):
                halo_copy(half, c, side).wait_send()


def per_device(field, mask, noise, lat_factor, lon_factor, time_tiles, amplitude, depth):
    hours, lats, lons = field.shape
    rows = hours * lats
    piece = rows // C // 16
    anywhere = pl.BlockSpec(memory_space=pl.ANY)
    vmem = pl.BlockSpec(memory_space=pltpu.VMEM)
    smem = pl.BlockSpec(memory_space=pltpu.SMEM)
    dma = pltpu.SemaphoreType.DMA
    result = pl.pallas_call(
        kernel,
        out_shape=pltpu.VMEM((rows, lons), F32),
        in_specs=[anywhere, anywhere, vmem, vmem, vmem, vmem, smem, smem],
        out_specs=vmem,
        scratch_shapes=[
            pltpu.VMEM((rows, lons), F32),
            pltpu.VMEM((rows, lons), jnp.int32),
            pltpu.VMEM((rows, 128), F32),
            pltpu.VMEM((rows, 128), F32),
            pltpu.VMEM((2, C, 16, piece, 128), F32),
            pltpu.VMEM((2, C, 16, piece, 128), F32),
            pltpu.VMEM((2, 3 * rows, 128), F32),
            pltpu.VMEM((2, rows, 128), F32),
            pltpu.VMEM((hours, 3 * hours), BF16),
            pltpu.VMEM((hours, 3 * hours), BF16),
            pltpu.VMEM((3 * hours, 256), BF16),
            pltpu.VMEM((3 * hours, 256), BF16),
            pltpu.VMEM((2, lons, lons), BF16),
            pltpu.VMEM((128, 256), BF16),
            dma((C,)), dma((C,)),
            dma((2, C)), dma((2, C)), dma((2, C)), dma((2, C)),
            dma((2, 2, C)), dma((2, 2, C)),
        ],
        compiler_params=pltpu.CompilerParams(
            collective_id=0, has_side_effects=True, vmem_limit_bytes=52 << 20
        ),
    )(
        field.reshape(rows, lons), mask.reshape(rows, lons), noise,
        lat_factor, lon_factor, time_tiles, amplitude, depth,
    )
    return result.reshape(hours, lats, lons)


def solution(mesh):
    spread = P("tm", "space", None)
    in_specs = (spread, spread, P("space", None), P(), P(), P(), P(), P())
    return jax.shard_map(
        per_device, mesh=mesh, in_specs=in_specs, out_specs=spread, check_vma=False
    )
```

```python
import jax
import jax.numpy as jnp
from jax import lax
from jax.experimental import pallas as pl
from jax.experimental.pallas import tpu as pltpu
from jax.sharding import PartitionSpec as P

MESH = pl.DeviceIdType.MESH
F32 = jnp.float32
BF16 = jnp.bfloat16
C = 4
HB = 128
OFFSETS = [
    (2, 2), (1, 2), (2, 1), (3, 2), (2, 3), (1, 1), (3, 3), (1, 3), (3, 1),
    (2, 0), (0, 2), (1, 0), (0, 1), (3, 0), (0, 3),
]


def split(x):
    hi = x.astype(BF16)
    return hi, (x - hi.astype(F32)).astype(BF16)


def dot(a, b):
    return jnp.dot(a, b, preferred_element_type=F32)


def kernel(
    field, mask, noise_in, lat_in, lon_in, tiles_in, amp_in, depth_in, out,
    fbuf, mbuf, first, mixed, r_buf, z_buf, wide, y_buf, wh, wl, xh, xl, lon2, lat2,
    noise, lat, lon, tiles, amp, depth, field_sem, mask_sem, small_sem, fwd_send, fwd_recv, back_send, back_recv, halo_send, halo_recv,
):
    t = lax.axis_index("tm")
    s = lax.axis_index("space")
    sz, sy = s // 4, s % 4
    peers = [lax.rem(sz + dz, 4) * 4 + lax.rem(sy + dy, 4) for dy, dz in OFFSETS]
    right, left = lax.rem(t + 1, 8), lax.rem(t + 7, 8)
    rows = fbuf.shape[0]
    chunk = rows // C
    piece = chunk // 16

    def load(c):
        part = pl.ds(c * chunk, chunk)
        return (
            pltpu.make_async_copy(field.at[part], fbuf.at[part], field_sem.at[c]),
            pltpu.make_async_copy(mask.at[part], mbuf.at[part], mask_sem.at[c]),
        )

    barrier = pltpu.get_barrier_semaphore()
    for peer in peers:
        pl.semaphore_signal(barrier, inc=1, device_id=(t, peer), device_id_type=MESH)
    for side in (left, right):
        pl.semaphore_signal(barrier, inc=1, device_id=(side, s), device_id_type=MESH)

    small = [
        pltpu.make_async_copy(source, target, small_sem.at[k])
        for k, (source, target) in enumerate(
            ((lon_in, lon), (lat_in, lat), (tiles_in, tiles), (amp_in, amp), (depth_in, depth), (noise_in, noise))
        )
    ]
    small[0].start()
    for c in range(C):
        for copy in load(c):
            copy.start()
    for copy in small[1:]:
        copy.start()

    small[0].wait()
    hi, lo = split(lon[...])
    lon2[0] = hi
    lon2[1] = lo

    def lon_product(c):
        for copy in load(c):
            copy.wait()
        part = pl.ds(pl.multiple_of(c * chunk, chunk), chunk)
        hi, lo = split(mbuf[part, :].astype(F32) * fbuf[part, :])
        x = dot(hi, lon2[0]) + dot(hi, lon2[1]) + dot(lo, lon2[0])
        first[part, :] = x[:, 0:128]
        wide[1, pl.ds(pl.multiple_of(rows + c * chunk, chunk), chunk), :] = x[:, 128:256]

    def send_forward(half, c):
        source = (first, mixed)[half]
        for peer in peers:
            pltpu.make_async_remote_copy(
                source.at[pl.ds((c * 16 + peer) * piece, piece)],
                r_buf.at[half, c, s],
                fwd_send.at[half, c],
                fwd_recv.at[half, c],
                device_id=(t, peer),
                device_id_type=MESH,
            ).start()
        pltpu.make_async_copy(
            source.at[pl.ds((c * 16 + s) * piece, piece)], r_buf.at[half, c, s], fwd_recv.at[half, c]
        ).start()

    def lat_product(half, c):
        got = r_buf.at[half, c]
        pltpu.make_async_copy(got, got, fwd_recv.at[half, c]).wait()
        for h in range(0, piece // 8, 2):
            x = jnp.concatenate(
                [r_buf[half, c, :, pl.ds((h + k) * 8, 8), :].reshape(128, 128) for k in range(2)], axis=1
            )
            hi, lo = split(x)
            y = dot(lat2[...], jnp.concatenate([hi, hi], axis=0)) + dot(lat2[:, 0:128], lo)
            for k in range(2):
                part = y[:, k * 128 : k * 128 + 128]
                z_buf[half, c, :, pl.ds((h + k) * 8, 8), :] = part.reshape(16, 8, 128)
        place = (c * 16 + s) * piece
        target = (wide.at[0, pl.ds(rows + place, piece)], y_buf.at[1, pl.ds(place, piece)])[half]
        for peer in peers:
            pltpu.make_async_remote_copy(
                z_buf.at[half, c, peer],
                target,
                back_send.at[half, c],
                back_recv.at[half, c],
                device_id=(t, peer),
                device_id_type=MESH,
            ).start()
        pltpu.make_async_copy(z_buf.at[half, c, s], target, back_recv.at[half, c]).start()

    def halo_copy(half, c, side):
        return pltpu.make_async_remote_copy(
            wide.at[half, pl.ds(rows + c * chunk, chunk)],
            wide.at[half, pl.ds(2 * side * rows + c * chunk, chunk)],
            halo_send.at[half, side, c],
            halo_recv.at[half, side, c],
            device_id=((right, left)[side], s),
            device_id_type=MESH,
        )

    def time_product(half):
        for c in range(C):
            for side in range(2):
                halo_copy(half, c, side).wait_recv()

        @pl.loop(0, 4)
        def _(p):
            for g in range(12):
                x = jnp.concatenate(
                    [wide[half, pl.ds(g * (HB * 8) + 2 * p + k, HB, stride=8), :] for k in range(2)], axis=1
                )
                hi, lo = split(x)
                xh[pl.ds(g * HB, HB), :] = hi
                xl[pl.ds(g * HB, HB), :] = lo
            x = dot(wh[...], xh[...]) + dot(wl[...], xh[...]) + dot(wh[...], xl[...])
            for k in range(2):
                every = pl.ds(2 * p + k, rows // 8, stride=8)
                part = x[:, k * 128 : k * 128 + 128]
                if half == 0:
                    y_buf[0, every, :] = part
                else:
                    mixed[every, :] = part

    def finish(half, c):
        part = pl.ds(pl.multiple_of(c * chunk, chunk), chunk)
        lanes = slice(half * 128, half * 128 + 128)
        tall = (chunk // 8, 8, 128)
        value = mbuf[part, lanes].astype(F32) * y_buf[half, part, :]
        value = value.reshape(tall) + noise[:, lanes][None] * fbuf[part, lanes].reshape(tall)
        out[part, lanes] = value.reshape(chunk, 128)

    lon_product(0)
    pl.semaphore_wait(barrier, len(peers) + 2)
    send_forward(0, 0)
    for side in range(2):
        halo_copy(1, 0, side).start()

    @pl.loop(1, C)
    def _(c):
        lon_product(c)
        send_forward(0, c)
        for side in range(2):
            halo_copy(1, c, side).start()

    for copy in small[1:]:
        copy.wait()
    hi, lo = split(lat[...])
    lat2[:, 0:128] = hi
    lat2[:, 128:256] = lo

    for j in range(12):
        for i in range(4):
            shift = j - 4 - i
            place, across = pl.ds(i * HB, HB), pl.ds(j * HB, HB)
            if abs(shift) > 4:
                wh[place, across] = jnp.zeros((HB, HB), BF16)
                wl[place, across] = jnp.zeros((HB, HB), BF16)
                continue
            to = t * 4 + i
            source = to + shift
            inside = (source >= 0) & (source <= 31)
            source = jnp.clip(source, 0, 31)
            keep = inside & (abs(shift) <= depth[jnp.minimum(to, source)])
            factor = jnp.where(keep, amp[to] * amp[source], 0.0)
            tile = tiles[abs(shift)]
            if shift < 0:
                tile = tile.T
            wh[place, across], wl[place, across] = split(factor * tile)

    @pl.loop(0, C)
    def _(c):
        lat_product(0, c)

    time_product(1)

    @pl.loop(0, C)
    def _(c):
        send_forward(1, c)

    @pl.loop(0, C)
    def _(c):
        got = wide.at[0, pl.ds(rows + c * chunk, chunk)]
        pltpu.make_async_copy(got, got, back_recv.at[0, c]).wait()
        for side in range(2):
            halo_copy(0, c, side).start()

    @pl.loop(0, C)
    def _(c):
        lat_product(1, c)

    time_product(0)

    @pl.loop(0, C)
    def _(c):
        finish(0, c)

    @pl.loop(0, C)
    def _(c):
        got = y_buf.at[1, pl.ds(c * chunk, chunk)]
        pltpu.make_async_copy(got, got, back_recv.at[1, c]).wait()
        finish(1, c)

    @pl.loop(0, C)
    def _(c):
        for half in range(2):
            sent = z_buf.at[half, c, pl.ds(0, 15)]
            pltpu.make_async_copy(sent, sent, fwd_send.at[half, c]).wait()
            pltpu.make_async_copy(sent, sent, back_send.at[half, c]).wait()
            for side in range(2):
                halo_copy(half, c, side).wait_send()


def per_device(field, mask, noise, lat_factor, lon_factor, time_tiles, amplitude, depth):
    hours, lats, lons = field.shape
    rows = hours * lats
    piece = rows // C // 16
    anywhere = pl.BlockSpec(memory_space=pl.ANY)
    vmem = pl.BlockSpec(memory_space=pltpu.VMEM)
    dma = pltpu.SemaphoreType.DMA
    result = pl.pallas_call(
        kernel,
        out_shape=pltpu.VMEM((rows, lons), F32),
        in_specs=[anywhere] * 8,
        out_specs=vmem,
        scratch_shapes=[
            pltpu.VMEM((rows, lons), F32),
            pltpu.VMEM((rows, lons), jnp.int32),
            pltpu.VMEM((rows, 128), F32),
            pltpu.VMEM((rows, 128), F32),
            pltpu.VMEM((2, C, 16, piece, 128), F32),
            pltpu.VMEM((2, C, 16, piece, 128), F32),
            pltpu.VMEM((2, 3 * rows, 128), F32),
            pltpu.VMEM((2, rows, 128), F32),
            pltpu.VMEM((hours, 3 * hours), BF16),
            pltpu.VMEM((hours, 3 * hours), BF16),
            pltpu.VMEM((3 * hours, 256), BF16),
            pltpu.VMEM((3 * hours, 256), BF16),
            pltpu.VMEM((2, lons, lons), BF16),
            pltpu.VMEM((128, 256), BF16),
            pltpu.VMEM(noise.shape, F32),
            pltpu.VMEM(lat_factor.shape, F32),
            pltpu.VMEM(lon_factor.shape, F32),
            pltpu.VMEM(time_tiles.shape, F32),
            pltpu.SMEM(amplitude.shape, F32),
            pltpu.SMEM(depth.shape, jnp.int32),
            dma((C,)), dma((C,)), dma((6,)),
            dma((2, C)), dma((2, C)), dma((2, C)), dma((2, C)),
            dma((2, 2, C)), dma((2, 2, C)),
        ],
        compiler_params=pltpu.CompilerParams(
            collective_id=0, has_side_effects=True, vmem_limit_bytes=52 << 20
        ),
    )(
        field.reshape(rows, lons), mask.reshape(rows, lons), noise,
        lat_factor, lon_factor, time_tiles, amplitude, depth,
    )
    return result.reshape(hours, lats, lons)


def solution(mesh):
    spread = P("tm", "space", None)
    in_specs = (spread, spread, P("space", None), P(), P(), P(), P(), P())
    return jax.shard_map(
        per_device, mesh=mesh, in_specs=in_specs, out_specs=spread, check_vma=False
    )
```

```python
import functools

import jax
import jax.numpy as jnp
from jax import lax
from jax.experimental import pallas as pl
from jax.experimental.pallas import tpu as pltpu
from jax.sharding import PartitionSpec as P

MESH = pl.DeviceIdType.MESH
F32 = jnp.float32
BF16 = jnp.bfloat16
C = 4
HB = 128
OFFSETS = [
    (2, 2), (1, 2), (2, 1), (3, 2), (2, 3), (1, 1), (3, 3), (1, 3), (3, 1),
    (2, 0), (0, 2), (1, 0), (0, 1), (3, 0), (0, 3),
]


def split(x):
    hi = x.astype(BF16)
    return hi, (x - hi.astype(F32)).astype(BF16)


def dot(a, b):
    return jnp.dot(a, b, preferred_element_type=F32)


def kernel(
    field, mask, noise_in, lat_in, lon_in, tiles_in, amp_in, depth_in, out,
    fbuf, mbuf, first, mixed, r_buf, z_buf, wide, y_buf, wh, wl, xh, xl, lon2, lat2,
    noise, lat, lon, tiles, amp, depth, field_sem, mask_sem, small_sem, fwd_send, fwd_recv, back_send, back_recv, halo_send, halo_recv,
):
    t = lax.axis_index("tm")
    s = lax.axis_index("space")
    sz, sy = s // 4, s % 4
    peers = [lax.rem(sz + dz, 4) * 4 + lax.rem(sy + dy, 4) for dy, dz in OFFSETS]
    right, left = lax.rem(t + 1, 8), lax.rem(t + 7, 8)
    rows = fbuf.shape[0]
    chunk = rows // C
    piece = chunk // 16

    def load(c):
        part = pl.ds(c * chunk, chunk)
        return (
            pltpu.make_async_copy(field.at[part], fbuf.at[part], field_sem.at[c]),
            pltpu.make_async_copy(mask.at[part], mbuf.at[part], mask_sem.at[c]),
        )

    barrier = pltpu.get_barrier_semaphore()
    for peer in peers:
        pl.semaphore_signal(barrier, inc=1, device_id=(t, peer), device_id_type=MESH)
    for side in (left, right):
        pl.semaphore_signal(barrier, inc=1, device_id=(side, s), device_id_type=MESH)

    small = [
        pltpu.make_async_copy(source, target, small_sem.at[k])
        for k, (source, target) in enumerate(
            ((lon_in, lon), (lat_in, lat), (tiles_in, tiles), (amp_in, amp), (depth_in, depth), (noise_in, noise))
        )
    ]
    small[0].start()
    for c in range(C):
        for copy in load(c):
            copy.start()
    for copy in small[1:]:
        copy.start()

    small[0].wait()
    hi, lo = split(lon[...])
    lon2[0] = hi
    lon2[1] = lo

    def lon_product(c):
        for copy in load(c):
            copy.wait()
        part = pl.ds(pl.multiple_of(c * chunk, chunk), chunk)
        hi, lo = split(mbuf[part, :].astype(F32) * fbuf[part, :])
        x = dot(hi, lon2[0]) + dot(hi, lon2[1]) + dot(lo, lon2[0])
        first[part, :] = x[:, 0:128]
        wide[1, pl.ds(pl.multiple_of(rows + c * chunk, chunk), chunk), :] = x[:, 128:256]

    def send_forward(half, c):
        source = (first, mixed)[half]
        for peer in peers:
            pltpu.make_async_remote_copy(
                source.at[pl.ds((c * 16 + peer) * piece, piece)],
                r_buf.at[half, c, s],
                fwd_send.at[half, c],
                fwd_recv.at[half, c],
                device_id=(t, peer),
                device_id_type=MESH,
            ).start()
        pltpu.make_async_copy(
            source.at[pl.ds((c * 16 + s) * piece, piece)], r_buf.at[half, c, s], fwd_recv.at[half, c]
        ).start()

    def lat_product(half, c):
        got = r_buf.at[half, c]
        pltpu.make_async_copy(got, got, fwd_recv.at[half, c]).wait()
        for h in range(0, piece // 8, 2):
            x = jnp.concatenate(
                [r_buf[half, c, :, pl.ds((h + k) * 8, 8), :].reshape(128, 128) for k in range(2)], axis=1
            )
            hi, lo = split(x)
            y = dot(lat2[...], jnp.concatenate([hi, hi], axis=0)) + dot(lat2[:, 0:128], lo)
            for k in range(2):
                part = y[:, k * 128 : k * 128 + 128]
                z_buf[half, c, :, pl.ds((h + k) * 8, 8), :] = part.reshape(16, 8, 128)
        place = (c * 16 + s) * piece
        target = (wide.at[0, pl.ds(rows + place, piece)], y_buf.at[1, pl.ds(place, piece)])[half]

        def send(peer):
            pltpu.make_async_remote_copy(
                z_buf.at[half, c, peer],
                target,
                back_send.at[half, c],
                back_recv.at[half, c],
                device_id=(t, peer),
                device_id_type=MESH,
            ).start()

        if half == 0:
            for peer in peers:
                send(peer)
        else:
            for turn in (True, False):
                for peer in peers:
                    early = (peer <= 1) | (peer == 3) | (peer == 4)
                    pl.when(early if turn else jnp.logical_not(early))(functools.partial(send, peer))

        pltpu.make_async_copy(z_buf.at[half, c, s], target, back_recv.at[half, c]).start()

    def halo_copy(half, c, side):
        return pltpu.make_async_remote_copy(
            wide.at[half, pl.ds(rows + c * chunk, chunk)],
            wide.at[half, pl.ds(2 * side * rows + c * chunk, chunk)],
            halo_send.at[half, side, c],
            halo_recv.at[half, side, c],
            device_id=((right, left)[side], s),
            device_id_type=MESH,
        )

    def time_product(half):
        for c in range(C):
            for side in range(2):
                halo_copy(half, c, side).wait_recv()

        @pl.loop(0, 4)
        def _(p):
            for g in range(12):
                x = jnp.concatenate(
                    [wide[half, pl.ds(g * (HB * 8) + 2 * p + k, HB, stride=8), :] for k in range(2)], axis=1
                )
                hi, lo = split(x)
                xh[pl.ds(g * HB, HB), :] = hi
                xl[pl.ds(g * HB, HB), :] = lo
            x = dot(wh[...], xh[...]) + dot(wl[...], xh[...]) + dot(wh[...], xl[...])
            for k in range(2):
                every = pl.ds(2 * p + k, rows // 8, stride=8)
                part = x[:, k * 128 : k * 128 + 128]
                if half == 0:
                    y_buf[0, every, :] = part
                else:
                    mixed[every, :] = part

    def finish(half, c):
        part = pl.ds(pl.multiple_of(c * chunk, chunk), chunk)
        lanes = slice(half * 128, half * 128 + 128)
        tall = (chunk // 8, 8, 128)
        value = mbuf[part, lanes].astype(F32) * y_buf[half, part, :]
        value = value.reshape(tall) + noise[:, lanes][None] * fbuf[part, lanes].reshape(tall)
        out[part, lanes] = value.reshape(chunk, 128)

    lon_product(0)
    pl.semaphore_wait(barrier, len(peers) + 2)
    send_forward(0, 0)
    for side in range(2):
        halo_copy(1, 0, side).start()

    @pl.loop(1, C)
    def _(c):
        lon_product(c)
        send_forward(0, c)
        for side in range(2):
            halo_copy(1, c, side).start()

    for copy in small[1:]:
        copy.wait()
    hi, lo = split(lat[...])
    lat2[:, 0:128] = hi
    lat2[:, 128:256] = lo

    for j in range(12):
        for i in range(4):
            shift = j - 4 - i
            place, across = pl.ds(i * HB, HB), pl.ds(j * HB, HB)
            if abs(shift) > 4:
                wh[place, across] = jnp.zeros((HB, HB), BF16)
                wl[place, across] = jnp.zeros((HB, HB), BF16)
                continue
            to = t * 4 + i
            source = to + shift
            inside = (source >= 0) & (source <= 31)
            source = jnp.clip(source, 0, 31)
            keep = inside & (abs(shift) <= depth[jnp.minimum(to, source)])
            factor = jnp.where(keep, amp[to] * amp[source], 0.0)
            tile = tiles[abs(shift)]
            if shift < 0:
                tile = tile.T
            wh[place, across], wl[place, across] = split(factor * tile)

    @pl.loop(0, C)
    def _(c):
        lat_product(0, c)

    time_product(1)

    @pl.loop(0, C)
    def _(c):
        send_forward(1, c)

    @pl.loop(0, C)
    def _(c):
        got = wide.at[0, pl.ds(rows + c * chunk, chunk)]
        pltpu.make_async_copy(got, got, back_recv.at[0, c]).wait()
        for side in range(2):
            halo_copy(0, c, side).start()

    @pl.loop(0, C)
    def _(c):
        lat_product(1, c)

    time_product(0)

    @pl.loop(0, C)
    def _(c):
        finish(0, c)

    @pl.loop(0, C)
    def _(c):
        got = y_buf.at[1, pl.ds(c * chunk, chunk)]
        pltpu.make_async_copy(got, got, back_recv.at[1, c]).wait()
        finish(1, c)

    @pl.loop(0, C)
    def _(c):
        for half in range(2):
            sent = z_buf.at[half, c, pl.ds(0, 15)]
            pltpu.make_async_copy(sent, sent, fwd_send.at[half, c]).wait()
            pltpu.make_async_copy(sent, sent, back_send.at[half, c]).wait()
            for side in range(2):
                halo_copy(half, c, side).wait_send()


def per_device(field, mask, noise, lat_factor, lon_factor, time_tiles, amplitude, depth):
    hours, lats, lons = field.shape
    rows = hours * lats
    piece = rows // C // 16
    anywhere = pl.BlockSpec(memory_space=pl.ANY)
    vmem = pl.BlockSpec(memory_space=pltpu.VMEM)
    dma = pltpu.SemaphoreType.DMA
    result = pl.pallas_call(
        kernel,
        out_shape=pltpu.VMEM((rows, lons), F32),
        in_specs=[anywhere] * 8,
        out_specs=vmem,
        scratch_shapes=[
            pltpu.VMEM((rows, lons), F32),
            pltpu.VMEM((rows, lons), jnp.int32),
            pltpu.VMEM((rows, 128), F32),
            pltpu.VMEM((rows, 128), F32),
            pltpu.VMEM((2, C, 16, piece, 128), F32),
            pltpu.VMEM((2, C, 16, piece, 128), F32),
            pltpu.VMEM((2, 3 * rows, 128), F32),
            pltpu.VMEM((2, rows, 128), F32),
            pltpu.VMEM((hours, 3 * hours), BF16),
            pltpu.VMEM((hours, 3 * hours), BF16),
            pltpu.VMEM((3 * hours, 256), BF16),
            pltpu.VMEM((3 * hours, 256), BF16),
            pltpu.VMEM((2, lons, lons), BF16),
            pltpu.VMEM((128, 256), BF16),
            pltpu.VMEM(noise.shape, F32),
            pltpu.VMEM(lat_factor.shape, F32),
            pltpu.VMEM(lon_factor.shape, F32),
            pltpu.VMEM(time_tiles.shape, F32),
            pltpu.SMEM(amplitude.shape, F32),
            pltpu.SMEM(depth.shape, jnp.int32),
            dma((C,)), dma((C,)), dma((6,)),
            dma((2, C)), dma((2, C)), dma((2, C)), dma((2, C)),
            dma((2, 2, C)), dma((2, 2, C)),
        ],
        compiler_params=pltpu.CompilerParams(
            collective_id=0, has_side_effects=True, vmem_limit_bytes=52 << 20
        ),
    )(
        field.reshape(rows, lons), mask.reshape(rows, lons), noise,
        lat_factor, lon_factor, time_tiles, amplitude, depth,
    )
    return result.reshape(hours, lats, lons)


def solution(mesh):
    spread = P("tm", "space", None)
    in_specs = (spread, spread, P("space", None), P(), P(), P(), P(), P())
    return jax.shard_map(
        per_device, mesh=mesh, in_specs=in_specs, out_specs=spread, check_vma=False
    )
```

```python
import functools

import jax
import jax.numpy as jnp
from jax import lax
from jax.experimental import pallas as pl
from jax.experimental.pallas import tpu as pltpu
from jax.sharding import PartitionSpec as P

MESH = pl.DeviceIdType.MESH
F32 = jnp.float32
BF16 = jnp.bfloat16
C = 4
HB = 128
OFFSETS = [
    (2, 2), (1, 2), (2, 1), (3, 2), (2, 3), (1, 1), (3, 3), (1, 3), (3, 1),
    (2, 0), (0, 2), (1, 0), (0, 1), (3, 0), (0, 3),
]


def split(x):
    hi = x.astype(BF16)
    return hi, (x - hi.astype(F32)).astype(BF16)


def dot(a, b):
    return jnp.dot(a, b, preferred_element_type=F32)


def kernel(
    field, mask, noise_in, lat_in, lon_in, tiles_in, amp_in, depth_in, out,
    fbuf, mbuf, first, mixed, r_buf, z_buf, wide, y_buf, wh, wl, xh, xl, lon2, lat2,
    noise, lat, lon, tiles, amp, depth, field_sem, mask_sem, small_sem, fwd_send, fwd_recv, back_send, back_recv, halo_send, halo_recv,
):
    t = lax.axis_index("tm")
    s = lax.axis_index("space")
    sz, sy = s // 4, s % 4
    peers = [lax.rem(sz + dz, 4) * 4 + lax.rem(sy + dy, 4) for dy, dz in OFFSETS]
    right, left = lax.rem(t + 1, 8), lax.rem(t + 7, 8)
    rows = fbuf.shape[0]
    chunk = rows // C
    piece = chunk // 16

    def load(c):
        part = pl.ds(c * chunk, chunk)
        return (
            pltpu.make_async_copy(field.at[part], fbuf.at[part], field_sem.at[c]),
            pltpu.make_async_copy(mask.at[part], mbuf.at[part], mask_sem.at[c]),
        )

    barrier = pltpu.get_barrier_semaphore()
    for peer in peers:
        pl.semaphore_signal(barrier, inc=1, device_id=(t, peer), device_id_type=MESH)
    for side in (left, right):
        pl.semaphore_signal(barrier, inc=1, device_id=(side, s), device_id_type=MESH)

    small = [
        pltpu.make_async_copy(source, target, small_sem.at[k])
        for k, (source, target) in enumerate(
            ((lon_in, lon), (lat_in, lat), (tiles_in, tiles), (amp_in, amp), (depth_in, depth), (noise_in, noise))
        )
    ]
    small[0].start()
    for c in range(C):
        for copy in load(c):
            copy.start()
    for copy in small[1:]:
        copy.start()

    small[0].wait()
    hi, lo = split(lon[...])
    lon2[0] = hi
    lon2[1] = lo

    def lon_product(c):
        for copy in load(c):
            copy.wait()
        part = pl.ds(pl.multiple_of(c * chunk, chunk), chunk)
        hi, lo = split(mbuf[part, :].astype(F32) * fbuf[part, :])
        x = dot(hi, lon2[0]) + dot(hi, lon2[1]) + dot(lo, lon2[0])
        first[part, :] = x[:, 0:128]
        wide[1, pl.ds(pl.multiple_of(rows + c * chunk, chunk), chunk), :] = x[:, 128:256]

    def send_forward(half, c):
        source = (first, mixed)[half]
        for peer in peers:
            pltpu.make_async_remote_copy(
                source.at[pl.ds((c * 16 + peer) * piece, piece)],
                r_buf.at[half, c, s],
                fwd_send.at[half, c],
                fwd_recv.at[half, c],
                device_id=(t, peer),
                device_id_type=MESH,
            ).start()
        pltpu.make_async_copy(
            source.at[pl.ds((c * 16 + s) * piece, piece)], r_buf.at[half, c, s], fwd_recv.at[half, c]
        ).start()

    def lat_product(half, c):
        got = r_buf.at[half, c]
        pltpu.make_async_copy(got, got, fwd_recv.at[half, c]).wait()
        for h in range(0, piece // 8, 2):
            x = jnp.concatenate(
                [r_buf[half, c, :, pl.ds((h + k) * 8, 8), :].reshape(128, 128) for k in range(2)], axis=1
            )
            hi, lo = split(x)
            y = dot(lat2[...], jnp.concatenate([hi, hi], axis=0)) + dot(lat2[:, 0:128], lo)
            for k in range(2):
                part = y[:, k * 128 : k * 128 + 128]
                z_buf[half, c, :, pl.ds((h + k) * 8, 8), :] = part.reshape(16, 8, 128)
        place = (c * 16 + s) * piece
        target = (wide.at[0, pl.ds(rows + place, piece)], y_buf.at[1, pl.ds(place, piece)])[half]

        def send(peer):
            pltpu.make_async_remote_copy(
                z_buf.at[half, c, peer],
                target,
                back_send.at[half, c],
                back_recv.at[half, c],
                device_id=(t, peer),
                device_id_type=MESH,
            ).start()

        if half == 0:
            for peer in peers:
                send(peer)
        else:
            for turn in (True, False):
                for peer in peers:
                    early = (peer <= 1) | (peer == 3) | (peer == 4)
                    pl.when(early if turn else jnp.logical_not(early))(functools.partial(send, peer))

        pltpu.make_async_copy(z_buf.at[half, c, s], target, back_recv.at[half, c]).start()

    def halo_copy(half, c, side):
        return pltpu.make_async_remote_copy(
            wide.at[half, pl.ds(rows + c * chunk, chunk)],
            wide.at[half, pl.ds(2 * side * rows + c * chunk, chunk)],
            halo_send.at[half, side, c],
            halo_recv.at[half, side, c],
            device_id=((right, left)[side], s),
            device_id_type=MESH,
        )

    def time_product(half):
        for c in range(C):
            for side in range(2):
                halo_copy(half, c, side).wait_recv()

        @pl.loop(0, 4)
        def _(p):
            for g in range(12):
                x = jnp.concatenate(
                    [wide[half, pl.ds(g * (HB * 8) + 2 * p + k, HB, stride=8), :] for k in range(2)], axis=1
                )
                hi, lo = split(x)
                xh[pl.ds(g * HB, HB), :] = hi
                xl[pl.ds(g * HB, HB), :] = lo
            x = dot(wh[...], xh[...]) + dot(wl[...], xh[...]) + dot(wh[...], xl[...])
            for k in range(2):
                every = pl.ds(2 * p + k, rows // 8, stride=8)
                part = x[:, k * 128 : k * 128 + 128]
                if half == 0:
                    y_buf[0, every, :] = part
                else:
                    mixed[every, :] = part

    def finish(half, c):
        part = pl.ds(pl.multiple_of(c * chunk, chunk), chunk)
        lanes = slice(half * 128, half * 128 + 128)
        tall = (chunk // 8, 8, 128)
        value = mbuf[part, lanes].astype(F32) * y_buf[half, part, :]
        value = value.reshape(tall) + noise[:, lanes][None] * fbuf[part, lanes].reshape(tall)
        out[part, lanes] = value.reshape(chunk, 128)

    lon_product(0)
    pl.semaphore_wait(barrier, len(peers) + 2)
    send_forward(0, 0)
    for side in range(2):
        halo_copy(1, 0, side).start()

    @pl.loop(1, C)
    def _(c):
        lon_product(c)
        send_forward(0, c)
        for side in range(2):
            halo_copy(1, c, side).start()

    for copy in small[1:]:
        copy.wait()
    hi, lo = split(lat[...])
    lat2[:, 0:128] = hi
    lat2[:, 128:256] = lo

    for j in range(12):
        for i in range(4):
            shift = j - 4 - i
            place, across = pl.ds(i * HB, HB), pl.ds(j * HB, HB)
            if abs(shift) > 4:
                wh[place, across] = jnp.zeros((HB, HB), BF16)
                wl[place, across] = jnp.zeros((HB, HB), BF16)
                continue
            to = t * 4 + i
            source = to + shift
            inside = (source >= 0) & (source <= 31)
            source = jnp.clip(source, 0, 31)
            keep = inside & (abs(shift) <= depth[jnp.minimum(to, source)])
            factor = jnp.where(keep, amp[to] * amp[source], 0.0)
            tile = tiles[abs(shift)]
            if shift < 0:
                tile = tile.T
            wh[place, across], wl[place, across] = split(factor * tile)

    @pl.loop(0, C)
    def _(c):
        lat_product(0, c)

    time_product(1)

    @pl.loop(0, C)
    def _(c):
        send_forward(1, c)

    @pl.loop(0, C)
    def _(c):
        got = wide.at[0, pl.ds(rows + c * chunk, chunk)]
        pltpu.make_async_copy(got, got, back_recv.at[0, c]).wait()
        for side in range(2):
            halo_copy(0, c, side).start()

    @pl.loop(0, C)
    def _(c):
        lat_product(1, c)

    time_product(0)

    @pl.loop(0, C)
    def _(c):
        finish(0, c)

    def sent(sems, half, c):
        part = z_buf.at[half, c, pl.ds(0, 15)]
        pltpu.make_async_copy(part, part, sems.at[half, c]).wait()

    @pl.loop(0, C)
    def _(c):
        for half in range(2):
            sent(fwd_send, half, c)
            for side in range(2):
                halo_copy(half, c, side).wait_send()
        sent(back_send, 0, c)

    @pl.loop(0, C)
    def _(c):
        got = y_buf.at[1, pl.ds(c * chunk, chunk)]
        pltpu.make_async_copy(got, got, back_recv.at[1, c]).wait()
        finish(1, c)

    @pl.loop(0, C)
    def _(c):
        sent(back_send, 1, c)


def per_device(field, mask, noise, lat_factor, lon_factor, time_tiles, amplitude, depth):
    hours, lats, lons = field.shape
    rows = hours * lats
    piece = rows // C // 16
    anywhere = pl.BlockSpec(memory_space=pl.ANY)
    vmem = pl.BlockSpec(memory_space=pltpu.VMEM)
    dma = pltpu.SemaphoreType.DMA
    result = pl.pallas_call(
        kernel,
        out_shape=pltpu.VMEM((rows, lons), F32),
        in_specs=[anywhere] * 8,
        out_specs=vmem,
        scratch_shapes=[
            pltpu.VMEM((rows, lons), F32),
            pltpu.VMEM((rows, lons), jnp.int32),
            pltpu.VMEM((rows, 128), F32),
            pltpu.VMEM((rows, 128), F32),
            pltpu.VMEM((2, C, 16, piece, 128), F32),
            pltpu.VMEM((2, C, 16, piece, 128), F32),
            pltpu.VMEM((2, 3 * rows, 128), F32),
            pltpu.VMEM((2, rows, 128), F32),
            pltpu.VMEM((hours, 3 * hours), BF16),
            pltpu.VMEM((hours, 3 * hours), BF16),
            pltpu.VMEM((3 * hours, 256), BF16),
            pltpu.VMEM((3 * hours, 256), BF16),
            pltpu.VMEM((2, lons, lons), BF16),
            pltpu.VMEM((128, 256), BF16),
            pltpu.VMEM(noise.shape, F32),
            pltpu.VMEM(lat_factor.shape, F32),
            pltpu.VMEM(lon_factor.shape, F32),
            pltpu.VMEM(time_tiles.shape, F32),
            pltpu.SMEM(amplitude.shape, F32),
            pltpu.SMEM(depth.shape, jnp.int32),
            dma((C,)), dma((C,)), dma((6,)),
            dma((2, C)), dma((2, C)), dma((2, C)), dma((2, C)),
            dma((2, 2, C)), dma((2, 2, C)),
        ],
        compiler_params=pltpu.CompilerParams(
            collective_id=0, has_side_effects=True, vmem_limit_bytes=52 << 20
        ),
    )(
        field.reshape(rows, lons), mask.reshape(rows, lons), noise,
        lat_factor, lon_factor, time_tiles, amplitude, depth,
    )
    return result.reshape(hours, lats, lons)


def solution(mesh):
    spread = P("tm", "space", None)
    in_specs = (spread, spread, P("space", None), P(), P(), P(), P(), P())
    return jax.shard_map(
        per_device, mesh=mesh, in_specs=in_specs, out_specs=spread, check_vma=False
    )
```

```python
import functools

import jax
import jax.numpy as jnp
from jax import lax
from jax.experimental import pallas as pl
from jax.experimental.pallas import tpu as pltpu
from jax.sharding import PartitionSpec as P

MESH = pl.DeviceIdType.MESH
F32 = jnp.float32
BF16 = jnp.bfloat16
C = 4
HB = 128
OFFSETS = [
    (2, 2), (1, 2), (3, 2), (0, 2), (2, 1), (1, 1), (3, 1), (0, 1),
    (2, 3), (1, 3), (3, 3), (0, 3), (2, 0), (1, 0), (3, 0),
]


def split(x):
    hi = x.astype(BF16)
    return hi, (x - hi.astype(F32)).astype(BF16)


def dot(a, b):
    return jnp.dot(a, b, preferred_element_type=F32)


def kernel(
    field, mask, noise_in, lat_in, lon_in, tiles_in, amp_in, depth_in, out,
    fbuf, mbuf, first, mixed, r_buf, z_buf, wide, y_buf, wh, wl, xh, xl, lon2, lat2,
    noise, lat, lon, tiles, amp, depth, field_sem, mask_sem, small_sem, fwd_send, fwd_recv, back_send, back_recv, halo_send, halo_recv,
):
    t = lax.axis_index("tm")
    s = lax.axis_index("space")
    sz, sy = s // 4, s % 4
    peers = [lax.rem(sz + dz, 4) * 4 + lax.rem(sy + dy, 4) for dy, dz in OFFSETS]
    right, left = lax.rem(t + 1, 8), lax.rem(t + 7, 8)
    rows = fbuf.shape[0]
    chunk = rows // C
    piece = chunk // 16

    def load(c):
        part = pl.ds(c * chunk, chunk)
        return (
            pltpu.make_async_copy(field.at[part], fbuf.at[part], field_sem.at[c]),
            pltpu.make_async_copy(mask.at[part], mbuf.at[part], mask_sem.at[c]),
        )

    barrier = pltpu.get_barrier_semaphore()
    for peer in peers:
        pl.semaphore_signal(barrier, inc=1, device_id=(t, peer), device_id_type=MESH)
    for side in (left, right):
        pl.semaphore_signal(barrier, inc=1, device_id=(side, s), device_id_type=MESH)

    small = [
        pltpu.make_async_copy(source, target, small_sem.at[k])
        for k, (source, target) in enumerate(
            ((lon_in, lon), (lat_in, lat), (tiles_in, tiles), (amp_in, amp), (depth_in, depth), (noise_in, noise))
        )
    ]
    small[0].start()
    for c in range(C):
        for copy in load(c):
            copy.start()
    for copy in small[1:]:
        copy.start()

    small[0].wait()
    hi, lo = split(lon[...])
    lon2[0] = hi
    lon2[1] = lo

    def lon_product(c):
        for copy in load(c):
            copy.wait()
        part = pl.ds(pl.multiple_of(c * chunk, chunk), chunk)
        hi, lo = split(mbuf[part, :].astype(F32) * fbuf[part, :])
        x = dot(hi, lon2[0]) + dot(hi, lon2[1]) + dot(lo, lon2[0])
        first[part, :] = x[:, 0:128]
        wide[1, pl.ds(pl.multiple_of(rows + c * chunk, chunk), chunk), :] = x[:, 128:256]

    def send_forward(half, c):
        source = (first, mixed)[half]
        for peer in peers:
            pltpu.make_async_remote_copy(
                source.at[pl.ds((c * 16 + peer) * piece, piece)],
                r_buf.at[half, c, s],
                fwd_send.at[half, c],
                fwd_recv.at[half, c],
                device_id=(t, peer),
                device_id_type=MESH,
            ).start()
        pltpu.make_async_copy(
            source.at[pl.ds((c * 16 + s) * piece, piece)], r_buf.at[half, c, s], fwd_recv.at[half, c]
        ).start()

    def lat_product(half, c):
        got = r_buf.at[half, c]
        pltpu.make_async_copy(got, got, fwd_recv.at[half, c]).wait()
        for h in range(0, piece // 8, 2):
            x = jnp.concatenate(
                [r_buf[half, c, :, pl.ds((h + k) * 8, 8), :].reshape(128, 128) for k in range(2)], axis=1
            )
            hi, lo = split(x)
            y = dot(lat2[...], jnp.concatenate([hi, hi], axis=0)) + dot(lat2[:, 0:128], lo)
            for k in range(2):
                part = y[:, k * 128 : k * 128 + 128]
                z_buf[half, c, :, pl.ds((h + k) * 8, 8), :] = part.reshape(16, 8, 128)
        place = (c * 16 + s) * piece
        target = (wide.at[0, pl.ds(rows + place, piece)], y_buf.at[1, pl.ds(place, piece)])[half]

        def send(peer):
            pltpu.make_async_remote_copy(
                z_buf.at[half, c, peer],
                target,
                back_send.at[half, c],
                back_recv.at[half, c],
                device_id=(t, peer),
                device_id_type=MESH,
            ).start()

        if half == 0:
            for peer in peers:
                send(peer)
        else:
            for turn in (True, False):
                for peer in peers:
                    early = (peer <= 1) | (peer == 3) | (peer == 4)
                    pl.when(early if turn else jnp.logical_not(early))(functools.partial(send, peer))

        pltpu.make_async_copy(z_buf.at[half, c, s], target, back_recv.at[half, c]).start()

    def halo_copy(half, c, side):
        return pltpu.make_async_remote_copy(
            wide.at[half, pl.ds(rows + c * chunk, chunk)],
            wide.at[half, pl.ds(2 * side * rows + c * chunk, chunk)],
            halo_send.at[half, side, c],
            halo_recv.at[half, side, c],
            device_id=((right, left)[side], s),
            device_id_type=MESH,
        )

    def time_product(half):
        for c in range(C):
            for side in range(2):
                halo_copy(half, c, side).wait_recv()

        @pl.loop(0, 4)
        def _(p):
            for g in range(12):
                x = jnp.concatenate(
                    [wide[half, pl.ds(g * (HB * 8) + 2 * p + k, HB, stride=8), :] for k in range(2)], axis=1
                )
                hi, lo = split(x)
                xh[pl.ds(g * HB, HB), :] = hi
                xl[pl.ds(g * HB, HB), :] = lo
            x = dot(wh[...], xh[...]) + dot(wl[...], xh[...]) + dot(wh[...], xl[...])
            for k in range(2):
                every = pl.ds(2 * p + k, rows // 8, stride=8)
                part = x[:, k * 128 : k * 128 + 128]
                if half == 0:
                    y_buf[0, every, :] = part
                else:
                    mixed[every, :] = part

    def finish(half, c):
        part = pl.ds(pl.multiple_of(c * chunk, chunk), chunk)
        lanes = slice(half * 128, half * 128 + 128)
        tall = (chunk // 8, 8, 128)
        value = mbuf[part, lanes].astype(F32) * y_buf[half, part, :]
        value = value.reshape(tall) + noise[:, lanes][None] * fbuf[part, lanes].reshape(tall)
        out[part, lanes] = value.reshape(chunk, 128)

    lon_product(0)
    pl.semaphore_wait(barrier, len(peers) + 2)
    send_forward(0, 0)
    for side in range(2):
        halo_copy(1, 0, side).start()

    @pl.loop(1, C)
    def _(c):
        lon_product(c)
        send_forward(0, c)
        for side in range(2):
            halo_copy(1, c, side).start()

    for copy in small[1:]:
        copy.wait()
    hi, lo = split(lat[...])
    lat2[:, 0:128] = hi
    lat2[:, 128:256] = lo

    for j in range(12):
        for i in range(4):
            shift = j - 4 - i
            place, across = pl.ds(i * HB, HB), pl.ds(j * HB, HB)
            if abs(shift) > 4:
                wh[place, across] = jnp.zeros((HB, HB), BF16)
                wl[place, across] = jnp.zeros((HB, HB), BF16)
                continue
            to = t * 4 + i
            source = to + shift
            inside = (source >= 0) & (source <= 31)
            source = jnp.clip(source, 0, 31)
            keep = inside & (abs(shift) <= depth[jnp.minimum(to, source)])
            factor = jnp.where(keep, amp[to] * amp[source], 0.0)
            tile = tiles[abs(shift)]
            if shift < 0:
                tile = tile.T
            wh[place, across], wl[place, across] = split(factor * tile)

    @pl.loop(0, C)
    def _(c):
        lat_product(0, c)

    time_product(1)

    @pl.loop(0, C)
    def _(c):
        send_forward(1, c)

    @pl.loop(0, C)
    def _(c):
        got = wide.at[0, pl.ds(rows + c * chunk, chunk)]
        pltpu.make_async_copy(got, got, back_recv.at[0, c]).wait()
        for side in range(2):
            halo_copy(0, c, side).start()

    @pl.loop(0, C)
    def _(c):
        lat_product(1, c)

    time_product(0)

    @pl.loop(0, C)
    def _(c):
        finish(0, c)

    @pl.loop(0, C)
    def _(c):
        got = y_buf.at[1, pl.ds(c * chunk, chunk)]
        pltpu.make_async_copy(got, got, back_recv.at[1, c]).wait()
        finish(1, c)

    @pl.loop(0, C)
    def _(c):
        for half in range(2):
            sent = z_buf.at[half, c, pl.ds(0, 15)]
            pltpu.make_async_copy(sent, sent, fwd_send.at[half, c]).wait()
            pltpu.make_async_copy(sent, sent, back_send.at[half, c]).wait()
            for side in range(2):
                halo_copy(half, c, side).wait_send()


def per_device(field, mask, noise, lat_factor, lon_factor, time_tiles, amplitude, depth):
    hours, lats, lons = field.shape
    rows = hours * lats
    piece = rows // C // 16
    anywhere = pl.BlockSpec(memory_space=pl.ANY)
    vmem = pl.BlockSpec(memory_space=pltpu.VMEM)
    dma = pltpu.SemaphoreType.DMA
    result = pl.pallas_call(
        kernel,
        out_shape=pltpu.VMEM((rows, lons), F32),
        in_specs=[anywhere] * 8,
        out_specs=vmem,
        scratch_shapes=[
            pltpu.VMEM((rows, lons), F32),
            pltpu.VMEM((rows, lons), jnp.int32),
            pltpu.VMEM((rows, 128), F32),
            pltpu.VMEM((rows, 128), F32),
            pltpu.VMEM((2, C, 16, piece, 128), F32),
            pltpu.VMEM((2, C, 16, piece, 128), F32),
            pltpu.VMEM((2, 3 * rows, 128), F32),
            pltpu.VMEM((2, rows, 128), F32),
            pltpu.VMEM((hours, 3 * hours), BF16),
            pltpu.VMEM((hours, 3 * hours), BF16),
            pltpu.VMEM((3 * hours, 256), BF16),
            pltpu.VMEM((3 * hours, 256), BF16),
            pltpu.VMEM((2, lons, lons), BF16),
            pltpu.VMEM((128, 256), BF16),
            pltpu.VMEM(noise.shape, F32),
            pltpu.VMEM(lat_factor.shape, F32),
            pltpu.VMEM(lon_factor.shape, F32),
            pltpu.VMEM(time_tiles.shape, F32),
            pltpu.SMEM(amplitude.shape, F32),
            pltpu.SMEM(depth.shape, jnp.int32),
            dma((C,)), dma((C,)), dma((6,)),
            dma((2, C)), dma((2, C)), dma((2, C)), dma((2, C)),
            dma((2, 2, C)), dma((2, 2, C)),
        ],
        compiler_params=pltpu.CompilerParams(
            collective_id=0, has_side_effects=True, vmem_limit_bytes=52 << 20
        ),
    )(
        field.reshape(rows, lons), mask.reshape(rows, lons), noise,
        lat_factor, lon_factor, time_tiles, amplitude, depth,
    )
    return result.reshape(hours, lats, lons)


def solution(mesh):
    spread = P("tm", "space", None)
    in_specs = (spread, spread, P("space", None), P(), P(), P(), P(), P())
    return jax.shard_map(
        per_device, mesh=mesh, in_specs=in_specs, out_specs=spread, check_vma=False
    )
```
